32 devices in a mesh: row: 4 (over y, x), col: 8 (over z, core).
Axes of the slice: x: 2, y: 2, z: 4, core: 2. Of those that a mesh axis runs over, the one named last changes fastest.
Arguments:
- a_terms: float32 [256, 16384], P('col', 'row'), may hold values from -6 to 6
- b_eval: float32 [512, 32768], P('col'), may hold values from -0.375 to 0.375
- term_slot: int32 [256], replicated, may hold values from 0 to 511, as said below
- term_sign: int32 [256], replicated, may hold values from -1 to 1, as said below
Outputs:
- joint: float32 [16384, 32768], P('row', 'col')
The draws below stay inside these ranges and needn't reach their ends.
Inputs may be any that keep to these rules, and one draw needn't show every extreme that they name: `term_slot`: entries are distinct. Slot s belongs to the evaluating device s // 64 along col. The numbers of terms held by devices d and d + 4 along col sum to exactly 64 for every d under 8 // 2; in every draw one device holds exactly 64, and slots 0 and 511 are always used. Rows of b_eval at slots that no term names are not used. `term_sign`: each entry is -1 or +1.
All inputs are finite; a program needn't handle non-finite values.
Results may differ from the reference program's by a relative error of at most 0.000071.
Values sent between devices are 32-bit elements; how exact they have to be, the bound alone decides.
No kernel may reach another device: no remote copies, remote signals or barrier semaphores. Data moves between devices by JAX's collectives and lax.ppermute only.
A program may use at most 192 MiB of HBM per device.

```python
import jax
import jax.numpy as jnp
from jax import lax

NA = 16384
NB = 32768
TERMS = 256
SLOTS = 64
SLOTS_ALL = 512
N_COL = 8


def draw_term_slot(key, part):
    first_key, second_key, third_key, fourth_key = jax.random.split(jax.random.fold_in(key, 7), 4)
    total_slots = SLOTS * N_COL
    half_way = N_COL // 2
    lower_counts = jax.random.randint(first_key, (half_way,), 1, SLOTS)
    busiest = jax.random.randint(second_key, (), 0, half_way - 1)
    lower_counts = jnp.where(jnp.arange(half_way) == busiest, SLOTS, lower_counts)
    counts = jnp.concatenate([lower_counts, SLOTS - lower_counts]).astype(jnp.int32)
    slot_ids = jnp.arange(total_slots, dtype=jnp.int32)
    shuffled = jax.random.permutation(third_key, total_slots).astype(jnp.int32)
    forced = (slot_ids == 0) | (slot_ids == total_slots - 1)
    score = jnp.where(forced, -1, shuffled).reshape(N_COL, SLOTS)
    rank_within = jnp.sum((score[:, None, :] < score[:, :, None]).astype(jnp.int32), axis=2)
    used = (rank_within < counts[:, None]).reshape(total_slots)
    ordered = jnp.argsort(jnp.where(used, slot_ids, total_slots + slot_ids), stable=True).astype(jnp.int32)
    chosen = ordered[:TERMS]
    term_order = jax.random.permutation(fourth_key, TERMS)
    return jnp.zeros((TERMS,), jnp.int32).at[term_order].set(chosen)


def draw_term_sign(key, part):
    coins = jax.random.randint(jax.random.fold_in(key, 11), (TERMS,), 0, 2)
    return (2 * coins - 1).astype(jnp.int32)


def block_scale(stream_key, dims, shards, least, high):
    def one(dim, shards_of):
        heights = jax.random.uniform(jax.random.fold_in(jax.random.fold_in(stream_key, 6), dim), (shards_of,), jnp.float32, least / len(shards), high / len(shards))
        return jnp.repeat(jnp.exp(heights), dims[dim] // shards_of).reshape((-1,) + (1,) * (len(dims) - dim - 1))

    gain = one(*shards[0])
    for cut in shards[1:]:
        gain = gain * one(*cut)
    return gain


def noise(key, extent, scale, limit, pieces=(), held_as=jnp.bfloat16):
    gain = block_scale(key, extent, pieces, -0.22, 0.18) if pieces else 1.0
    result = jax.random.normal(key, extent, jnp.float32) * scale * gain
    return jnp.minimum(jnp.maximum(result, -limit), limit).astype(held_as)


def setup_inputs(seed: int = 0) -> dict:
    key_list = jax.random.split(jax.random.key(seed), 5)
    a_terms = noise(key_list[0], (TERMS, NA), 1.0, 6.0, ((0, 8), (1, 4)), jnp.float32)
    b_eval = noise(key_list[1], (SLOTS_ALL, NB), TERMS ** -0.5, 0.375, ((0, 8),), jnp.float32)
    term_slot = draw_term_slot(jax.random.fold_in(key_list[4], 71), 0)
    term_sign = draw_term_sign(jax.random.fold_in(key_list[4], 71), 0)
    return {"a_terms": a_terms, "b_eval": b_eval, "term_slot": term_slot, "term_sign": term_sign}


def reference(a_terms, b_eval, term_slot, term_sign):
    b_terms = jnp.take(b_eval, term_slot, axis=0)
    signed = b_terms * term_sign.astype(b_terms.dtype)[:, None]
    return lax.dot_general(a_terms, signed, (((0,), (0,)), ((), ())), precision=lax.Precision.HIGHEST, preferred_element_type=jnp.float32)
```

```python
import jax
import jax.numpy as jnp
from jax import lax
from jax.sharding import PartitionSpec as P


def contract(left, right):
    return lax.dot_general(
        left,
        right,
        (((0,), (0,)), ((), ())),
        precision=lax.Precision.HIGH,
        preferred_element_type=jnp.float32,
    )


def solution(mesh):
    rows, cols = mesh.shape["row"], mesh.shape["col"]

    def shards(a_terms, b_eval, term_slot, term_sign):
        slots = b_eval.shape[0]
        part = b_eval.shape[1] // (rows * cols)
        mine = lax.dynamic_index_in_dim(b_eval.reshape(slots, cols, rows, part), lax.axis_index("row"), 2, keepdims=False)
        b_slots = lax.all_to_all(mine.transpose(1, 0, 2), "col", split_axis=0, concat_axis=0, tiled=True)
        b_slots = b_slots.reshape(cols * slots, part)
        signed = jnp.take(b_slots, term_slot, axis=0) * term_sign.astype(jnp.float32)[:, None]
        signed = lax.all_gather(signed, "row", axis=1, tiled=True)
        a_whole = lax.all_gather(a_terms, "col", axis=0, tiled=True)
        return contract(a_whole, signed)

    return jax.shard_map(
        shards,
        mesh=mesh,
        in_specs=(P("col", "row"), P("col", None), P(), P()),
        out_specs=P("row", "col"),
        check_vma=False,
    )
```

```python
import jax
import jax.numpy as jnp
from jax import lax
from jax.experimental import pallas as pl
from jax.experimental.pallas import tpu as pltpu
from jax.sharding import PartitionSpec as P

BF16, F32 = jnp.bfloat16, jnp.float32
VMEM_BYTES = 48 << 20


def halves(x):
    high = x.astype(BF16)
    return high, (x - high.astype(F32)).astype(BF16)


def dot(left, right):
    return jnp.dot(left, right, preferred_element_type=F32)


def cost(flops, moved):
    return pl.CostEstimate(flops=flops, bytes_accessed=moved, transcendentals=0)


def cut_blocks(b_eval, starts, widths):
    slots, cols = b_eval.shape[0], starts.shape[0]
    shapes = [jax.ShapeDtypeStruct((cols, slots, w), F32) for w in widths]

    def kernel(starts_ref, b_ref, *refs):
        outs, sems = refs[:-1], refs[-1]
        copies = []
        offset = 0
        for chunk, w in enumerate(widths):
            for q in range(cols):
                start = pl.multiple_of(starts_ref[q] + offset, 128)
                copies.append(
                    pltpu.make_async_copy(b_ref.at[:, pl.ds(start, w)], outs[chunk].at[q], sems.at[len(copies)])
                )
            offset += w
        for copy in copies:
            copy.start()
        for copy in copies:
            copy.wait()

    return pl.pallas_call(
        kernel,
        in_specs=[pl.BlockSpec(memory_space=pltpu.SMEM), pl.BlockSpec(memory_space=pl.ANY)],
        out_specs=[pl.BlockSpec(memory_space=pltpu.VMEM)] * len(shapes),
        out_shape=shapes,
        scratch_shapes=[pltpu.SemaphoreType.DMA((len(shapes) * cols,))],
        cost_estimate=cost(0, 8 * cols * slots * sum(widths)),
        name="cut_blocks",
    )(starts, b_eval)


def pack(blocks, select, at, w):
    cols, slots, _ = blocks.shape
    terms = select.shape[0]
    tile = min(w, 256)

    def kernel(select_ref, block_ref, out_ref):
        high, low = halves(block_ref[...].reshape(cols * slots, tile))
        out_ref[...] = dot(select_ref[...], high) + dot(select_ref[...], low)

    return pl.pallas_call(
        kernel,
        grid=(w // tile,),
        in_specs=[
            pl.BlockSpec(select.shape, lambda g: (0, 0)),
            pl.BlockSpec((cols, slots, tile), lambda g: (0, 0, at // tile + g)),
        ],
        out_specs=pl.BlockSpec((terms, tile), lambda g: (0, g)),
        out_shape=jax.ShapeDtypeStruct((terms, w), F32),
        cost_estimate=cost(4 * cols * slots * w * terms, 4 * (cols * slots + terms) * w),
        name="pack",
    )(select, blocks)


def split_a(parts):
    held, bins = parts[0].shape
    terms, tile = held * len(parts), min(bins, 1024)

    def kernel(*refs):
        high_ref, low_ref = refs[len(parts) :]
        for n in range(len(parts)):
            at = slice(n * held, (n + 1) * held)
            high_ref[:, at], low_ref[:, at] = halves(refs[n][...].T)

    return pl.pallas_call(
        kernel,
        grid=(bins // tile,),
        in_specs=[pl.BlockSpec((held, tile), lambda i: (0, i))] * len(parts),
        out_specs=[pl.BlockSpec((tile, terms), lambda i: (i, 0))] * 2,
        out_shape=[jax.ShapeDtypeStruct((bins, terms), BF16)] * 2,
        compiler_params=pltpu.CompilerParams(vmem_limit_bytes=VMEM_BYTES),
        cost_estimate=cost(0, 8 * bins * terms),
        name="split_a",
    )(*parts)


def product(high, low, pieces, places, joint, columns):
    bins, terms = high.shape
    count, w = len(pieces), pieces[0].shape[1]
    tile = min(bins, (1 << 21) // w)
    fresh = joint is None

    def kernel(places_ref, high_ref, low_ref, *refs):
        out_ref, b_high, b_low = refs[-3:]

        @pl.when(pl.program_id(1) == 0)
        def _():
            for p in range(count):
                @pl.when(pl.program_id(0) == p)
                def _():
                    b_high[...], b_low[...] = halves(refs[p][...])

        a_high, a_low = high_ref[...], low_ref[...]
        out_ref[...] = dot(a_high, b_high[...]) + dot(a_high, b_low[...]) + dot(a_low, b_high[...])

    row = lambda j, i, places_ref: (i, 0)
    whole = lambda j, i, places_ref: (0, 0)
    return pl.pallas_call(
        kernel,
        grid_spec=pltpu.PrefetchScalarGridSpec(
            num_scalar_prefetch=1,
            grid=(count, bins // tile),
            in_specs=[pl.BlockSpec((tile, terms), row)] * 2
            + [pl.BlockSpec((terms, w), whole)] * count
            + ([] if fresh else [pl.BlockSpec(memory_space=pl.ANY)]),
            out_specs=pl.BlockSpec((tile, w), lambda j, i, places_ref: (i, places_ref[j])),
            scratch_shapes=[pltpu.VMEM((terms, w), BF16)] * 2,
        ),
        out_shape=jax.ShapeDtypeStruct((bins, columns), F32),
        input_output_aliases={} if fresh else {3 + count: 0},
        compiler_params=pltpu.CompilerParams(vmem_limit_bytes=VMEM_BYTES),
        cost_estimate=cost(6 * bins * terms * count * w, 4 * bins * count * w),
        name="product",
    )(places, high, low, *pieces, *([] if fresh else [joint]))


def after(values, *earlier):
    return lax.optimization_barrier((values, earlier))[0]


def solution(mesh):
    rows, cols = mesh.shape["row"], mesh.shape["col"]

    def shards(a_terms, b_eval, term_slot, term_sign):
        slots, wide = b_eval.shape
        per = wide // cols
        part = per // rows
        if rows == 4 and part % 1024 == 0:
            crossings = [[part // 2], [part // 2]]
        else:
            crossings = [[part]]
        r = lax.axis_index("row")

        starts = (jnp.arange(cols) * per + r * part).astype(jnp.int32)
        cut = cut_blocks(b_eval, starts, [sum(c) for c in crossings])
        a_whole = lax.all_gather(a_terms, "col", axis=0, tiled=True)
        used = term_slot[:, None] == jnp.arange(cols * slots)[None, :]
        select = jnp.where(used, term_sign[:, None], 0).astype(BF16)
        high, low = split_a([a_whole])

        mine, places, pieces, offset, blocks = [], [], [], 0, None
        for c, widths in enumerate(crossings):
            block = cut[c] if blocks is None else after(cut[c], blocks)
            blocks = lax.all_to_all(block, "col", 0, 0, tiled=True)
            if c and c == len(crossings) - 1:
                blocks = after(blocks, high, low)
            at = 0
            for w in widths:
                mine.append(pack(blocks, select, at, w))
                if rows == 4:
                    pieces.append([mine[-1]] + [lax.ppermute(mine[-1], "row", [(q, q ^ n) for q in range(4)]) for n in (1, 2, 3)])
                    quarter = jnp.stack([r, r ^ 1, r ^ 2, r ^ 3])
                else:
                    pieces.append(list(lax.all_gather(mine[-1], "row")))
                    quarter = jnp.arange(rows)
                places.append((quarter * (part // w) + offset // w).astype(jnp.int32))
                at, offset = at + w, offset + w
        joint = None
        for n in range(len(mine)):
            ready = pieces[n] if n == len(mine) - 1 else after(pieces[n], mine[n + 1])
            joint = product(high, low, ready, places[n], joint, per)
        return joint

    return jax.shard_map(
        shards,
        mesh=mesh,
        in_specs=(P("col", "row"), P("col", None), P(), P()),
        out_specs=P("row", "col"),
        check_vma=False,
    )
```

```python
import jax
import jax.numpy as jnp
from jax import lax
from jax.experimental import pallas as pl
from jax.experimental.pallas import tpu as pltpu
from jax.sharding import PartitionSpec as P

BF16, F32 = jnp.bfloat16, jnp.float32
VMEM_BYTES = 48 << 20


def halves(x):
    high = x.astype(BF16)
    return high, (x - high.astype(F32)).astype(BF16)


def dot(left, right):
    return jnp.dot(left, right, preferred_element_type=F32)


def cost(flops, moved):
    return pl.CostEstimate(flops=flops, bytes_accessed=moved, transcendentals=0)


def cut_blocks(b_eval, cols, rows, widths):
    slots, per = b_eval.shape[0], b_eval.shape[1] // cols
    shapes = [jax.ShapeDtypeStruct((cols, slots, w), F32) for w in widths]

    def kernel(b_ref, *refs):
        mine = lax.axis_index("row") * (per // rows)
        outs, sems = refs[:-1], refs[-1]
        copies = []
        offset = 0
        for chunk, w in enumerate(widths):
            for q in range(cols):
                start = pl.multiple_of(mine + (q * per + offset), 128)
                copies.append(
                    pltpu.make_async_copy(b_ref.at[:, pl.ds(start, w)], outs[chunk].at[q], sems.at[len(copies)])
                )
            offset += w
        for copy in copies:
            copy.start()
        for copy in copies:
            copy.wait()

    return pl.pallas_call(
        kernel,
        in_specs=[pl.BlockSpec(memory_space=pl.ANY)],
        out_specs=[pl.BlockSpec(memory_space=pltpu.VMEM)] * len(shapes),
        out_shape=shapes,
        scratch_shapes=[pltpu.SemaphoreType.DMA((len(shapes) * cols,))],
        cost_estimate=cost(0, 8 * cols * slots * sum(widths)),
        name="cut_blocks",
    )(b_eval)


def pack(blocks, select, at, w):
    cols, slots, _ = blocks.shape
    terms = select.shape[0]
    tile = min(w, 256)

    def kernel(select_ref, block_ref, out_ref):
        high, low = halves(block_ref[...].reshape(cols * slots, tile))
        out_ref[...] = dot(select_ref[...], high) + dot(select_ref[...], low)

    return pl.pallas_call(
        kernel,
        grid=(w // tile,),
        in_specs=[
            pl.BlockSpec(select.shape, lambda g: (0, 0)),
            pl.BlockSpec((cols, slots, tile), lambda g: (0, 0, at // tile + g)),
        ],
        out_specs=pl.BlockSpec((terms, tile), lambda g: (0, g)),
        out_shape=jax.ShapeDtypeStruct((terms, w), F32),
        cost_estimate=cost(4 * cols * slots * w * terms, 4 * (cols * slots + terms) * w),
        name="pack",
    )(select, blocks)


def split_a(parts):
    held, bins = parts[0].shape
    terms, tile = held * len(parts), min(bins, 1024)

    def kernel(*refs):
        high_ref, low_ref = refs[len(parts) :]
        for n in range(len(parts)):
            at = slice(n * held, (n + 1) * held)
            high_ref[:, at], low_ref[:, at] = halves(refs[n][...].T)

    return pl.pallas_call(
        kernel,
        grid=(bins // tile,),
        in_specs=[pl.BlockSpec((held, tile), lambda i: (0, i))] * len(parts),
        out_specs=[pl.BlockSpec((tile, terms), lambda i: (i, 0))] * 2,
        out_shape=[jax.ShapeDtypeStruct((bins, terms), BF16)] * 2,
        compiler_params=pltpu.CompilerParams(vmem_limit_bytes=VMEM_BYTES),
        cost_estimate=cost(0, 8 * bins * terms),
        name="split_a",
    )(*parts)


def product(high, low, pieces, places, joint, columns):
    bins, terms = high.shape
    count, w = len(pieces), pieces[0].shape[1]
    tile = min(bins, (1 << 21) // w)
    fresh = joint is None

    def kernel(places_ref, high_ref, low_ref, *refs):
        out_ref, b_high, b_low = refs[-3:]

        @pl.when(pl.program_id(1) == 0)
        def _():
            for p in range(count):
                @pl.when(pl.program_id(0) == p)
                def _():
                    b_high[...], b_low[...] = halves(refs[p][...])

        a_high, a_low = high_ref[...], low_ref[...]
        out_ref[...] = dot(a_high, b_high[...]) + dot(a_high, b_low[...]) + dot(a_low, b_high[...])

    row = lambda j, i, places_ref: (i, 0)
    whole = lambda j, i, places_ref: (0, 0)
    return pl.pallas_call(
        kernel,
        grid_spec=pltpu.PrefetchScalarGridSpec(
            num_scalar_prefetch=1,
            grid=(count, bins // tile),
            in_specs=[pl.BlockSpec((tile, terms), row)] * 2
            + [pl.BlockSpec((terms, w), whole)] * count
            + ([] if fresh else [pl.BlockSpec(memory_space=pl.ANY)]),
            out_specs=pl.BlockSpec((tile, w), lambda j, i, places_ref: (i, places_ref[j])),
            scratch_shapes=[pltpu.VMEM((terms, w), BF16)] * 2,
        ),
        out_shape=jax.ShapeDtypeStruct((bins, columns), F32),
        input_output_aliases={} if fresh else {3 + count: 0},
        compiler_params=pltpu.CompilerParams(vmem_limit_bytes=VMEM_BYTES),
        cost_estimate=cost(6 * bins * terms * count * w, 4 * bins * count * w),
        name="product",
    )(places, high, low, *pieces, *([] if fresh else [joint]))


def after(values, *earlier):
    return lax.optimization_barrier((values, earlier))[0]


def solution(mesh):
    rows, cols = mesh.shape["row"], mesh.shape["col"]

    def shards(a_terms, b_eval, term_slot, term_sign):
        slots, wide = b_eval.shape
        per = wide // cols
        part = per // rows
        if rows == 4 and part % 1024 == 0:
            crossings = [[part // 2], [part // 2]]
        else:
            crossings = [[part]]
        r = lax.axis_index("row")

        cut = cut_blocks(b_eval, cols, rows, [sum(c) for c in crossings])
        a_whole = lax.all_gather(a_terms, "col", axis=0, tiled=True)
        used = term_slot[:, None] == jnp.arange(cols * slots)[None, :]
        select = jnp.where(used, term_sign[:, None], 0).astype(BF16)
        high, low = split_a([a_whole])

        crossed = []
        for block in cut:
            crossed.append(lax.all_to_all(after(block, crossed), "col", 0, 0, tiled=True))

        if len(cut) == 1:
            pieces = list(lax.all_gather(pack(crossed[0], select, 0, part), "row"))
            return product(high, low, pieces, jnp.arange(rows, dtype=jnp.int32), None, per)

        def share(x):
            return [lax.ppermute(x, "row", [(q, q ^ way) for q in range(4)]) for way in (1, 2, 3)]

        w = part // 2
        quarter = (2 * jnp.stack([r, r ^ 1, r ^ 2, r ^ 3])).astype(jnp.int32)
        first = pack(crossed[0], select, 0, w)
        shared = share(first)
        joint = product(high, low, [first], quarter[:1], None, per)
        second = pack(after(crossed[1], joint), select, 0, w)
        shared_second = share(second)
        places = jnp.concatenate([quarter[1:], quarter[:1] + 1])
        joint = product(high, low, after(shared, second) + [second], places, joint, per)
        return product(high, low, shared_second, quarter[1:] + 1, joint, per)

    return jax.shard_map(
        shards,
        mesh=mesh,
        in_specs=(P("col", "row"), P("col", None), P(), P()),
        out_specs=P("row", "col"),
        check_vma=False,
    )
```

```python
import jax
import jax.numpy as jnp
from jax import lax
from jax.experimental import pallas as pl
from jax.experimental.pallas import tpu as pltpu
from jax.sharding import PartitionSpec as P

BF16, F32 = jnp.bfloat16, jnp.float32
VMEM_BYTES = 48 << 20


def halves(x):
    high = x.astype(BF16)
    return high, (x - high.astype(F32)).astype(BF16)


def dot(left, right):
    return jnp.dot(left, right, preferred_element_type=F32)


def cost(flops, moved):
    return pl.CostEstimate(flops=flops, bytes_accessed=moved, transcendentals=0)


def cut_blocks(b_eval, cols, rows, widths, begin=0):
    slots, per = b_eval.shape[0], b_eval.shape[1] // cols
    shapes = [jax.ShapeDtypeStruct((cols, slots, w), F32) for w in widths]

    def kernel(b_ref, *refs):
        mine = lax.axis_index("row") * (per // rows)
        outs, sems = refs[:-1], refs[-1]
        copies = []
        offset = begin
        for chunk, w in enumerate(widths):
            for q in range(cols):
                start = pl.multiple_of(mine + (q * per + offset), 128)
                copies.append(
                    pltpu.make_async_copy(b_ref.at[:, pl.ds(start, w)], outs[chunk].at[q], sems.at[len(copies)])
                )
            offset += w
        for copy in copies:
            copy.start()
        for copy in copies:
            copy.wait()

    return pl.pallas_call(
        kernel,
        in_specs=[pl.BlockSpec(memory_space=pl.ANY)],
        out_specs=[pl.BlockSpec(memory_space=pltpu.VMEM)] * len(shapes),
        out_shape=shapes,
        scratch_shapes=[pltpu.SemaphoreType.DMA((len(shapes) * cols,))],
        cost_estimate=cost(0, 8 * cols * slots * sum(widths)),
        name="cut_blocks",
    )(b_eval)


def pack(blocks, select, at, w):
    cols, slots, _ = blocks.shape
    terms = select.shape[0]
    tile = min(w, 256)

    def kernel(select_ref, block_ref, out_ref):
        high, low = halves(block_ref[...].reshape(cols * slots, tile))
        out_ref[...] = dot(select_ref[...], high) + dot(select_ref[...], low)

    return pl.pallas_call(
        kernel,
        grid=(w // tile,),
        in_specs=[
            pl.BlockSpec(select.shape, lambda g: (0, 0)),
            pl.BlockSpec((cols, slots, tile), lambda g: (0, 0, at // tile + g)),
        ],
        out_specs=pl.BlockSpec((terms, tile), lambda g: (0, g)),
        out_shape=jax.ShapeDtypeStruct((terms, w), F32),
        cost_estimate=cost(4 * cols * slots * w * terms, 4 * (cols * slots + terms) * w),
        name="pack",
    )(select, blocks)


def split_a(parts):
    held, bins = parts[0].shape
    terms, tile = held * len(parts), min(bins, 1024)

    def kernel(*refs):
        high_ref, low_ref = refs[len(parts) :]
        for n in range(len(parts)):
            at = slice(n * held, (n + 1) * held)
            high_ref[:, at], low_ref[:, at] = halves(refs[n][...].T)

    return pl.pallas_call(
        kernel,
        grid=(bins // tile,),
        in_specs=[pl.BlockSpec((held, tile), lambda i: (0, i))] * len(parts),
        out_specs=[pl.BlockSpec((tile, terms), lambda i: (i, 0))] * 2,
        out_shape=[jax.ShapeDtypeStruct((bins, terms), BF16)] * 2,
        compiler_params=pltpu.CompilerParams(vmem_limit_bytes=VMEM_BYTES),
        cost_estimate=cost(0, 8 * bins * terms),
        name="split_a",
    )(*parts)


def product(high, low, pieces, places, joint, columns):
    bins, terms = high.shape
    count, w = len(pieces), pieces[0].shape[1]
    tile = min(bins, (1 << 21) // w)
    fresh = joint is None

    def kernel(places_ref, high_ref, low_ref, *refs):
        out_ref, b_high, b_low = refs[-3:]

        @pl.when(pl.program_id(1) == 0)
        def _():
            for p in range(count):
                @pl.when(pl.program_id(0) == p)
                def _():
                    b_high[...], b_low[...] = halves(refs[p][...])

        a_high, a_low = high_ref[...], low_ref[...]
        out_ref[...] = dot(a_high, b_high[...]) + dot(a_high, b_low[...]) + dot(a_low, b_high[...])

    row = lambda j, i, places_ref: (i, 0)
    whole = lambda j, i, places_ref: (0, 0)
    return pl.pallas_call(
        kernel,
        grid_spec=pltpu.PrefetchScalarGridSpec(
            num_scalar_prefetch=1,
            grid=(count, bins // tile),
            in_specs=[pl.BlockSpec((tile, terms), row)] * 2
            + [pl.BlockSpec((terms, w), whole)] * count
            + ([] if fresh else [pl.BlockSpec(memory_space=pl.ANY)]),
            out_specs=pl.BlockSpec((tile, w), lambda j, i, places_ref: (i, places_ref[j])),
            scratch_shapes=[pltpu.VMEM((terms, w), BF16)] * 2,
        ),
        out_shape=jax.ShapeDtypeStruct((bins, columns), F32),
        input_output_aliases={} if fresh else {3 + count: 0},
        compiler_params=pltpu.CompilerParams(vmem_limit_bytes=VMEM_BYTES),
        cost_estimate=cost(6 * bins * terms * count * w, 4 * bins * count * w),
        name="product",
    )(places, high, low, *pieces, *([] if fresh else [joint]))


def after(values, *earlier):
    return lax.optimization_barrier((values, earlier))[0]


def solution(mesh):
    rows, cols = mesh.shape["row"], mesh.shape["col"]

    def shards(a_terms, b_eval, term_slot, term_sign):
        slots, wide = b_eval.shape
        per = wide // cols
        part = per // rows
        if rows == 4 and part % 1024 == 0:
            crossings = [[part // 2], [part // 2]]
        else:
            crossings = [[part]]
        r = lax.axis_index("row")

        cut = [cut_blocks(b_eval, cols, rows, [part // len(crossings)], n * part // len(crossings))[0] for n in range(len(crossings))]
        a_whole = lax.all_gather(a_terms, "col", axis=0, tiled=True)
        used = term_slot[:, None] == jnp.arange(cols * slots)[None, :]
        select = jnp.where(used, term_sign[:, None], 0).astype(BF16)
        high, low = split_a([a_whole])

        crossed = []
        for block in cut:
            crossed.append(lax.all_to_all(after(block, crossed), "col", 0, 0, tiled=True))

        if len(cut) == 1:
            pieces = list(lax.all_gather(pack(crossed[0], select, 0, part), "row"))
            return product(high, low, pieces, jnp.arange(rows, dtype=jnp.int32), None, per)

        def share(x):
            return [lax.ppermute(x, "row", [(q, q ^ way) for q in range(4)]) for way in (1, 2, 3)]

        w = part // 2
        quarter = (2 * jnp.stack([r, r ^ 1, r ^ 2, r ^ 3])).astype(jnp.int32)
        first = pack(crossed[0], select, 0, w)
        shared = share(first)
        joint = product(high, low, [first], quarter[:1], None, per)
        second = pack(after(crossed[1], joint), select, 0, w)
        shared_second = share(second)
        places = jnp.concatenate([quarter[1:], quarter[:1] + 1])
        joint = product(high, low, after(shared, second) + [second], places, joint, per)
        return product(high, low, shared_second, quarter[1:] + 1, joint, per)

    return jax.shard_map(
        shards,
        mesh=mesh,
        in_specs=(P("col", "row"), P("col", None), P(), P()),
        out_specs=P("row", "col"),
        check_vma=False,
    )
```
